32 devices in a mesh: band: 8 (over y, x, core), bus: 4 (over z).
Axes of the slice: x: 2, y: 2, z: 4, core: 2. Of those that a mesh axis runs over, the one named last changes fastest.
Arguments:
- dispatch0: float32 [64, 5120], P(None, ('band', 'bus')), may hold values from 0 to 1
- cost_lin: float32 [5120], P(('band', 'bus')), may hold values from -1 to 1
- cost_quad: float32 [5120], P(('band', 'bus')), may hold values from 0.5 to 4
- gen_max: float32 [5120], P(('band', 'bus')), may hold values from 0.5 to 2
- bus_map: int32 [5120], P(('band', 'bus')), may hold values from 0 to 98303, as said below
- demand: float32 [64, 4, 24576], P(None, 'bus', 'band'), may hold values from -6 to 6
- ptdf: float32 [2048, 98304], P('band', 'bus'), may hold values from -0.01953125 to 0.01953125
- line_price0: float32 [64, 2048], P(None, 'band'), may hold values from -3 to 3
- flow_max: float32 [2048], P('band'), may hold values from 0.3 to 3
Outputs:
- dispatch: float32 [64, 5120], P(None, ('band', 'bus'))
- line_price: float32 [64, 2048], P(None, 'band')
The draws below stay inside these ranges and needn't reach their ends.
Inputs may be any that keep to these rules, and one draw needn't show every extreme that they name: `bus_map`: call bus 24576 * j + 3072 * i + k with 0 <= k < 3072 a bus of sub-block (i, j). Among the 160 generators of one aligned block (generators 160 * d to 160 * d + 159), at most 6 are sited in one sub-block, and one sub-block holds exactly 6 generators of every block.
All inputs are finite; a program needn't handle non-finite values.
Results may differ from the reference program's by a relative error of at most 0.0003.
Values sent between devices are 32-bit elements; how exact they have to be, the bound alone decides.
A program may use at most 128 MiB of HBM per device.

```python
import math
import jax
import jax.numpy as jnp
from jax import lax

BUS_DEV = 24576
GEN_DEV = 160
S = 64
ITERS = 2
SUB = 3072
BUSES = 98304
LINES = 2048
GENS = 5120
CAP = 6
N_BUS = 4
DEVICES = 32


def draw_bus_map(key, part):
    hot_key, rest_key = jax.random.split(jax.random.fold_in(key, 7))
    hot = jax.random.randint(hot_key, (), 0, DEVICES).astype(jnp.int32)

    def one_block(block_key):
        first_key, second_key, third_key = jax.random.split(block_key, 3)
        slots = jax.random.permutation(first_key, (DEVICES - 1) * CAP)[:GEN_DEV - CAP].astype(jnp.int32)
        other = slots // CAP
        other = other + (other >= hot).astype(jnp.int32)
        owner = jnp.concatenate([jnp.full((CAP,), hot, jnp.int32), other])
        owner = jax.random.permutation(second_key, owner).astype(jnp.int32)
        within = jax.random.randint(third_key, (GEN_DEV,), 0, SUB).astype(jnp.int32)
        return owner % N_BUS * BUS_DEV + owner // N_BUS * SUB + within
    block_keys = jax.random.split(rest_key, DEVICES)
    return jax.vmap(one_block)(block_keys).reshape(-1).astype(jnp.int32)


def levels(stream_key, dims, pieces, smallest, top_value):
    gain = 1.0
    for axis_at, shards_of in pieces:
        heights = jax.random.uniform(jax.random.fold_in(jax.random.fold_in(stream_key, 6), axis_at), (shards_of,), jnp.float32, smallest / len(pieces), top_value / len(pieces))
        gain = gain * jnp.repeat(jnp.exp(heights), dims[axis_at] // shards_of).reshape((-1,) + (1,) * (len(dims) - 1 - axis_at))
    return gain


def noise(own_key, extent, width, reach, cuts=(), dtype=jnp.bfloat16):
    array = jax.random.normal(own_key, extent, jnp.float32) * width
    if len(cuts) > 0:
        array = levels(own_key, extent, cuts, -0.22, 0.18) * array
    return jnp.clip(array, min=-reach, max=reach).astype(dtype)


def setup_inputs(seed: int = 0) -> dict:
    splits = jax.random.split(jax.random.key(seed), 10)
    dispatch0 = jnp.clip(1.0 * jax.random.uniform(splits[0], (S, GENS), jnp.float32) ** levels(splits[0], (S, GENS), ((1, 32),), -0.2, 0.2), 0.0, 1.0)
    cost_lin = jnp.clip(jax.random.uniform(splits[1], (GENS,), jnp.float32, -1.0, 1.0) * levels(splits[1], (GENS,), ((0, 32),), -0.4, 0.0), -1.0, 1.0)
    cost_quad = jnp.clip(jnp.exp(math.log(4.0) - 2.0794415 * jax.random.uniform(splits[2], (GENS,), jnp.float32) ** levels(splits[2], (GENS,), ((0, 32),), -0.2, 0.2)), 0.5, 4.0)
    gen_max = jnp.clip(0.5 + 1.5 * jax.random.uniform(splits[3], (GENS,), jnp.float32) ** levels(splits[3], (GENS,), ((0, 32),), -0.2, 0.2), 0.5, 2.0)
    bus_map = draw_bus_map(jax.random.fold_in(splits[9], 71), 0)
    demand = noise(splits[5], (S, N_BUS, BUS_DEV), 1.0, 6.0, ((1, 4), (2, 8)), jnp.float32)
    ptdf = noise(splits[6], (LINES, BUSES), BUSES ** -0.5, 0.01953125, ((0, 8), (1, 4)), jnp.float32)
    line_price0 = noise(splits[7], (S, LINES), 0.5, 3.0, ((1, 8),), jnp.float32)
    flow_max = jnp.clip(jnp.exp(math.log(3.0) - 2.3025851 * jax.random.uniform(splits[8], (LINES,), jnp.float32) ** levels(splits[8], (LINES,), ((0, 8),), -0.2, 0.2)), 0.3, 3.0)
    return dict(dispatch0=dispatch0, cost_lin=cost_lin, cost_quad=cost_quad, gen_max=gen_max, bus_map=bus_map, demand=demand, ptdf=ptdf, line_price0=line_price0, flow_max=flow_max)


primal_step = 0.5
dual_step = 1.0


def reference(dispatch0, cost_lin, cost_quad, gen_max, bus_map, demand, ptdf, line_price0, flow_max):
    dispatch = dispatch0
    line_price = line_price0
    load = demand.reshape(S, BUSES)
    bound = dual_step * flow_max
    for iteration in range(ITERS):
        injection = jnp.zeros((S, BUSES), jnp.float32).at[:, bus_map].add(dispatch) - load
        flow = jnp.dot(injection, ptdf.T, precision=lax.Precision.HIGHEST, preferred_element_type=jnp.float32)
        trial = line_price + dual_step * flow
        price_next = trial - jnp.clip(trial, -bound, bound)
        reflected = 2.0 * price_next - line_price
        bus_price = jnp.dot(reflected, ptdf, precision=lax.Precision.HIGHEST, preferred_element_type=jnp.float32)
        unit_price = bus_price[:, bus_map]
        dispatch = jnp.clip((dispatch - primal_step * (cost_lin[None, :] + unit_price)) / (1.0 + primal_step * cost_quad[None, :]), 0.0, gen_max[None, :])
        line_price = price_next
    return dispatch, line_price
```

```python
import functools
import jax
import jax.numpy as jnp
from jax import lax
from jax.experimental import pallas as pl
from jax.experimental.pallas import tpu as pltpu
from jax.sharding import PartitionSpec as P

ITERS = 2
ROWS = 8
LANES = 128
MESH = pl.DeviceIdType.MESH

primal_step = 0.5
dual_step = 1.0

NT = (((1,), (1,)), ((), ()))
NN = (((1,), (0,)), ((), ()))


def owner_slots(bus_map, bus_width, sub_width, bus_count):
    block = bus_map // bus_width
    within = bus_map % bus_width
    owner = within // sub_width * bus_count + block
    local = within % sub_width
    same = owner[:, None] == owner[None, :]
    earlier = lax.broadcasted_iota(jnp.int32, same.shape, 0) > lax.broadcasted_iota(
        jnp.int32, same.shape, 1
    )
    rank = jnp.sum((same & earlier).astype(jnp.int32), axis=1)
    return (owner * ROWS + rank, local)


def split(x):
    hi = x.astype(jnp.bfloat16)
    lo = (x - hi.astype(jnp.float32)).astype(jnp.bfloat16)
    return hi, lo


def dot(a, b, dims):
    return lax.dot_general(a, b, dims, preferred_element_type=jnp.float32)


def flip(i, m, bits):
    r = i
    for b in range(bits):
        w = 1 << b
        ib = (i // w) % 2
        mb = (m // w) % 2
        r = r + w * mb * (1 - 2 * ib)
    return r


def market_kernel(
    nb, nz, cap, depth, kt,
    pack_ref, dem_ref, ptdf_ref, lp0_ref, fmax_ref,
    ret_ref, lp_ref,
    pin, slots, dem, pbuf, acc1, acc2, ghi, glo, lf, zbuf, dbuf, pps, ppr, rout, rin,
    dloc_sem, p_sem, a_send, a_recv, dem_send, dem_recv, fw_send,
    z_send, z_recv, d_send, d_recv, pp_send, pp_recv, r_send, r_recv,
):
    i = lax.axis_index("band")
    j = lax.axis_index("bus")
    n = nb * nz
    me = i * nz + j
    bits = nb.bit_length() - 1
    scen = lp0_ref.shape[0]
    lines = lp0_ref.shape[1]
    sub = dem_ref.shape[1]
    s_count = n * cap
    partner = i + 1 - 2 * (i % 2)

    def pcopy(m):
        o = flip(i, m, bits)
        return pltpu.make_async_copy(
            ptdf_ref.at[:, pl.ds(pl.multiple_of(o * sub, LANES), sub)],
            pbuf.at[m % depth],
            p_sem.at[m % depth],
        )

    @pl.loop(0, depth)
    def _(m):
        pcopy(m).start()

    dloc = pltpu.make_async_copy(dem_ref, dem.at[i], dloc_sem.at[0])
    dloc.start()
    ploc = pltpu.make_async_copy(pack_ref.at[me], pin.at[me], dloc_sem.at[1])
    ploc.start()

    barrier = pltpu.get_barrier_semaphore()

    @pl.loop(1, n)
    def _(k):
        d = (me + k) % n
        pl.semaphore_signal(barrier, inc=1, device_id=(d // nz, d % nz), device_id_type=MESH)

    pl.semaphore_wait(barrier, n - 1)

    def acopy(d, s):
        return pltpu.make_async_remote_copy(
            src_ref=pack_ref.at[d], dst_ref=pin.at[s], send_sem=a_send.at[d], recv_sem=a_recv.at[s],
            device_id=(d // nz, d % nz), device_id_type=MESH,
        )

    @pl.loop(1, n)
    def _(k):
        acopy((me + k) % n, me).start()

    def dcopy(m):
        to = flip(i, m, bits)
        return pltpu.make_async_remote_copy(
            src_ref=dem_ref, dst_ref=dem.at[i], send_sem=dem_send.at[m], recv_sem=dem_recv.at[i],
            device_id=(to, j), device_id_type=MESH,
        )

    def fcopy(m):
        o = flip(i, m, bits)
        return pltpu.make_async_remote_copy(
            src_ref=dem.at[o], dst_ref=dem.at[o], send_sem=fw_send.at[m], recv_sem=dem_recv.at[o],
            device_id=(partner, j), device_id_type=MESH,
        )

    dcopy(1).start()
    for m in range(2, nb, 2):
        dcopy(m).start()

    @pl.loop(1, n)
    def _(k):
        s = (me + k) % n
        acopy(s, s).wait_recv()

    ploc.wait()
    if cap == ROWS:
        slots[...] = pin[...].reshape(s_count, LANES)
    else:
        for d in range(n):
            slots[d * cap:(d + 1) * cap, :] = pin[d, 0:cap, :]
    pack_t = slots[...].T
    lin = pack_t[scen:scen + 1, :]
    quad = pack_t[scen + 1:scen + 2, :]
    gmax = pack_t[scen + 2:scen + 3, :]
    dbuf[0, i] = pack_t[0:scen, :]

    def gcopy(it, m):
        to = flip(i, m, bits)
        return pltpu.make_async_remote_copy(
            src_ref=dbuf.at[it, i], dst_ref=dbuf.at[it, i],
            send_sem=d_send.at[it, m], recv_sem=d_recv.at[it, i],
            device_id=(to, j), device_id_type=MESH,
        )

    def gwait(it, m):
        o = flip(i, m, bits)
        return pltpu.make_async_remote_copy(
            src_ref=dbuf.at[it, o], dst_ref=dbuf.at[it, o],
            send_sem=d_send.at[it, m], recv_sem=d_recv.at[it, o],
            device_id=(o, j), device_id_type=MESH,
        )

    @pl.loop(1, nb)
    def _(m):
        gcopy(0, m).start()

    dloc.wait()
    lf[...] = jnp.zeros_like(lf)
    lane = lax.broadcasted_iota(jnp.int32, (s_count, LANES), 1)
    at_lane = lax.broadcasted_iota(jnp.int32, (s_count, kt), 1).astype(jnp.float32) + 1.0

    @pl.loop(0, nb)
    def _(m):
        o = flip(i, m, bits)

        @pl.when(m > 0)
        def _():
            fcopy(m).wait_recv()

        @pl.when((m > 0) & (m % 2 == 0))
        def _():
            fcopy(m).start()

        pcopy(m).wait()
        codes = jnp.sum(jnp.where(lane == LANES - nb + o, slots[...], 0.0), axis=1, keepdims=True)
        for t in range(sub // kt):
            cols = slice(t * kt, (t + 1) * kt)
            ph, plo = split(pbuf[m % depth, :, cols])
            dh, dl = split(dem[o, :, cols])
            oh = jnp.where(at_lane == codes - float(t * kt), 1.0, 0.0).astype(jnp.bfloat16)
            one = dot(jnp.concatenate([dh, dl, oh], axis=0), ph, NT)
            two = dot(jnp.concatenate([dh, oh], axis=0), plo, NT)
            if t == 0:
                acc1[...] = one
                acc2[...] = two
            else:
                acc1[...] += one
                acc2[...] += two
        lf[...] += (acc1[scen:2 * scen, :] + acc2[0:scen, :]) + acc1[0:scen, :]
        ghi[o] = acc1[2 * scen:2 * scen + s_count, :].astype(jnp.bfloat16)
        glo[o] = acc2[scen:scen + s_count, :].astype(jnp.bfloat16)

        @pl.when(m + depth < nb)
        def _():
            pcopy(m + depth).start()

    price = lp0_ref[...]
    bound = dual_step * fmax_ref[...]

    for it in range(ITERS):
        zbuf[it, j] = -lf[...]

        def add_flow(m, it=it):
            o = flip(i, m, bits)
            dh, dl = split(dbuf[it, o])
            both = dot(jnp.concatenate([dh, dl], axis=0), ghi[o], NN)
            zbuf[it, j] += both[scen:, :] + dot(dh, glo[o], NN) + both[0:scen, :]

        add_flow(0)

        @pl.loop(1, nb)
        def _(m, it=it):
            gwait(it, m).wait_recv()
            add_flow(m)

        def zcopy(k, it=it):
            to = (j + k) % nz
            return pltpu.make_async_remote_copy(
                src_ref=zbuf.at[it, j], dst_ref=zbuf.at[it, j],
                send_sem=z_send.at[it, k], recv_sem=z_recv.at[it, j],
                device_id=(i, to), device_id_type=MESH,
            )

        def zwait(k, it=it):
            o = (j + k) % nz
            return pltpu.make_async_remote_copy(
                src_ref=zbuf.at[it, o], dst_ref=zbuf.at[it, o],
                send_sem=z_send.at[it, k], recv_sem=z_recv.at[it, o],
                device_id=(i, o), device_id_type=MESH,
            )

        for k in range(1, nz):
            zcopy(k).start()
        for k in range(1, nz):
            zwait(k).wait_recv()
        flow = zbuf[it, 0]
        for k in range(1, nz):
            flow = flow + zbuf[it, k]
        trial = price + dual_step * flow
        price_next = trial - jnp.clip(trial, -bound, bound)
        reflected = 2.0 * price_next - price
        price = price_next

        rh, rl = split(reflected)
        rhl = jnp.concatenate([rh, rl], axis=0)

        def slot_price(o):
            both = dot(rhl, ghi[o], NT)
            return both[scen:, :] + dot(rh, glo[o], NT) + both[0:scen, :]

        def ppcopy(m, it=it):
            o = flip(i, m, bits)
            return pltpu.make_async_remote_copy(
                src_ref=pps.at[o], dst_ref=ppr.at[it, i],
                send_sem=pp_send.at[it, m], recv_sem=pp_recv.at[it, i],
                device_id=(o, j), device_id_type=MESH,
            )

        def ppwait(m, it=it):
            o = flip(i, m, bits)
            return pltpu.make_async_remote_copy(
                src_ref=pps.at[o], dst_ref=ppr.at[it, o],
                send_sem=pp_send.at[it, m], recv_sem=pp_recv.at[it, o],
                device_id=(o, j), device_id_type=MESH,
            )

        @pl.loop(0, nb - 1)
        def _(k):
            m = nb - 1 - k
            o = flip(i, m, bits)
            pps[o] = slot_price(o)
            ppcopy(m).start()

        ppr[it, i] = slot_price(i)

        @pl.loop(1, nb)
        def _(m):
            ppwait(m).wait_recv()
            ppcopy(m).wait_send()

        unit = ppr[it, 0]
        for s in range(1, nb):
            unit = unit + ppr[it, s]
        held = dbuf[it, i]
        held = jnp.clip(
            (held - primal_step * (lin + unit)) / (1.0 + primal_step * quad), 0.0, gmax
        )
        if it < ITERS - 1:
            dbuf[it + 1, i] = held

            @pl.loop(1, nb)
            def _(m, it=it):
                gcopy(it + 1, m).start()

    lp_ref[...] = price
    back = jnp.concatenate([held, jnp.zeros((LANES - scen, s_count), jnp.float32)], axis=0).T
    if cap == ROWS:
        rout[...] = back.reshape(n, ROWS, LANES)
    else:
        rout[...] = jnp.zeros_like(rout)
        slots[...] = back
        for d in range(n):
            rout[d, 0:cap, :] = slots[d * cap:(d + 1) * cap, :]

    def rcopy(d, s):
        return pltpu.make_async_remote_copy(
            src_ref=rout.at[d], dst_ref=rin.at[s], send_sem=r_send.at[d], recv_sem=r_recv.at[s],
            device_id=(d // nz, d % nz), device_id_type=MESH,
        )

    @pl.loop(1, n)
    def _(k):
        rcopy((me + k) % n, me).start()

    dcopy(1).wait_send()
    for m in range(2, nb, 2):
        dcopy(m).wait_send()
        fcopy(m).wait_send()

    @pl.loop(1, nb)
    def _(m):
        for it in range(ITERS):
            gcopy(it, m).wait_send()

    for it in range(ITERS):
        for k in range(1, nz):
            pltpu.make_async_remote_copy(
                src_ref=zbuf.at[it, j], dst_ref=zbuf.at[it, j],
                send_sem=z_send.at[it, k], recv_sem=z_recv.at[it, j],
                device_id=(i, (j + k) % nz), device_id_type=MESH,
            ).wait_send()

    ret_ref[me] = rout[me]

    @pl.loop(1, n)
    def _(k):
        d = (me + k) % n
        acopy(d, d).wait_send()
        rcopy(d, d).wait_recv()
        rcopy(d, d).wait_send()
        ret_ref[d] = rin[d]


def on_device(
    dispatch0, cost_lin, cost_quad, gen_max, bus_map, demand, ptdf, line_price0, flow_max
):
    nb = lax.axis_size("band")
    nz = lax.axis_size("bus")
    n = nb * nz
    gens = bus_map.shape[0]
    scen = dispatch0.shape[0]
    sub = demand.shape[2]
    lines = ptdf.shape[0]
    cap = (gens + n - 1) // n + 1
    while n * cap % LANES:
        cap += 1
    s_count = n * cap
    assert cap <= ROWS and scen + 4 + nb <= LANES and nb & (nb - 1) == 0
    target, local = owner_slots(bus_map, ptdf.shape[1], sub, nz)
    body = jnp.concatenate(
        [
            dispatch0,
            cost_lin[None, :],
            cost_quad[None, :],
            gen_max[None, :],
            (local + 1).astype(jnp.float32)[None, :],
        ],
        axis=0,
    ).T
    rows = jnp.zeros((n * ROWS, scen + 4), jnp.float32).at[target].set(body).reshape(n, ROWS, scen + 4)
    codes = rows[:, :, scen + 3].reshape(nb, nz, ROWS).transpose(1, 2, 0)
    codes = jnp.broadcast_to(codes[None], (nb, nz, ROWS, nb)).reshape(n, ROWS, nb)
    pad = jnp.zeros((n, ROWS, LANES - nb - scen - 4), jnp.float32)
    pack = jnp.concatenate([rows, pad, codes], axis=2)

    depth = min(nb, 8)
    kt = sub
    while kt > 1024:
        kt //= 2
    if sub % kt or kt % LANES:
        kt = sub
    if sub % 1024 == 0:
        kt = 1024
    f32, bf16 = jnp.float32, jnp.bfloat16
    vmem = pl.BlockSpec(memory_space=pltpu.VMEM)
    dma = pltpu.SemaphoreType.DMA
    ret, line_price = pl.pallas_call(
        functools.partial(market_kernel, nb, nz, cap, depth, kt),
        out_shape=(
            jax.ShapeDtypeStruct((n, ROWS, LANES), f32),
            jax.ShapeDtypeStruct((scen, lines), f32),
        ),
        in_specs=[vmem, vmem, pl.BlockSpec(memory_space=pl.ANY), vmem, vmem],
        out_specs=(vmem, vmem),
        scratch_shapes=[
            pltpu.VMEM((n, ROWS, LANES), f32),
            pltpu.VMEM((s_count, LANES), f32),
            pltpu.VMEM((nb, scen, sub), f32),
            pltpu.VMEM((depth, lines, sub), f32),
            pltpu.VMEM((2 * scen + s_count, lines), f32),
            pltpu.VMEM((scen + s_count, lines), f32),
            pltpu.VMEM((nb, s_count, lines), bf16),
            pltpu.VMEM((nb, s_count, lines), bf16),
            pltpu.VMEM((scen, lines), f32),
            pltpu.VMEM((ITERS, nz, scen, lines), f32),
            pltpu.VMEM((ITERS, nb, scen, s_count), f32),
            pltpu.VMEM((nb, scen, s_count), f32),
            pltpu.VMEM((ITERS, nb, scen, s_count), f32),
            pltpu.VMEM((n, ROWS, LANES), f32),
            pltpu.VMEM((n, ROWS, LANES), f32),
            dma((2,)), dma((depth,)),
            dma((n,)), dma((n,)),
            dma((nb,)), dma((nb,)), dma((nb,)),
            dma((ITERS, nz)), dma((ITERS, nz)),
            dma((ITERS, nb)), dma((ITERS, nb)),
            dma((ITERS, nb)), dma((ITERS, nb)),
            dma((n,)), dma((n,)),
        ],
        compiler_params=pltpu.CompilerParams(
            collective_id=0, has_side_effects=True, vmem_limit_bytes=60 * 1024 * 1024
        ),
        name="market",
    )(pack, demand[:, 0, :], ptdf, line_price0, flow_max[None, :])
    dispatch = ret.reshape(n * ROWS, LANES)[target][:, :scen].T
    return (dispatch, line_price)


def solution(mesh):
    in_specs = (
        P(None, ("band", "bus")),
        P(("band", "bus")),
        P(("band", "bus")),
        P(("band", "bus")),
        P(("band", "bus")),
        P(None, "bus", "band"),
        P("band", "bus"),
        P(None, "band"),
        P("band"),
    )
    out_specs = (P(None, ("band", "bus")), P(None, "band"))
    return jax.shard_map(
        on_device, mesh=mesh, in_specs=in_specs, out_specs=out_specs, check_vma=False
    )
```

```python
import functools
import jax
import jax.numpy as jnp
from jax import lax
from jax.experimental import pallas as pl
from jax.experimental.pallas import tpu as pltpu
from jax.sharding import PartitionSpec as P

ITERS = 2
ROWS = 8
LANES = 128
MESH = pl.DeviceIdType.MESH

primal_step = 0.5
dual_step = 1.0

NT = (((1,), (1,)), ((), ()))
NN = (((1,), (0,)), ((), ()))


def split(x):
    hi = x.astype(jnp.bfloat16)
    lo = (x - hi.astype(jnp.float32)).astype(jnp.bfloat16)
    return hi, lo


def dot(a, b, dims):
    return lax.dot_general(a, b, dims, preferred_element_type=jnp.float32)


def flip(i, m, bits):
    r = i
    for b in range(bits):
        w = 1 << b
        ib = (i // w) % 2
        mb = (m // w) % 2
        r = r + w * mb * (1 - 2 * ib)
    return r


def market_kernel(
    nb, nz, cap, depth, kt,
    disp_ref, par_ref, bus_ref, dem_ref, ptdf_ref, lp0_ref, fmax_ref,
    out_ref, lp_ref,
    pack, pin, slots, dem, pbuf, acc1, acc2, ghi, glo, lf, zbuf, dbuf, pps, ppx, ppr, rout, rin,
    dloc_sem, p_sem, a_send, a_recv, dem_send, dem_recv, fw_send, fw_recv, rel_send,
    z_send, z_recv, d_send, d_recv, df_send, px_send, px_recv, pp_send, pp_recv, r_send, r_recv,
):
    i = lax.axis_index("band")
    j = lax.axis_index("bus")
    n = nb * nz
    me = i * nz + j
    bits = nb.bit_length() - 1
    scen = lp0_ref.shape[0]
    lines = lp0_ref.shape[1]
    sub = dem_ref.shape[2]
    gens = disp_ref.shape[1]
    relay = nb == 8
    half = scen // 2
    s_count = n * cap
    partner = i + 1 - 2 * (i % 2)

    def pcopy(m):
        o = flip(i, m, bits)
        return pltpu.make_async_copy(
            ptdf_ref.at[:, pl.ds(pl.multiple_of(o * sub, LANES), sub)],
            pbuf.at[m % depth],
            p_sem.at[m % depth],
        )

    @pl.loop(0, depth)
    def _(m):
        pcopy(m).start()

    dloc = pltpu.make_async_copy(dem_ref.at[:, 0, :], dem.at[i], dloc_sem.at[0])
    dloc.start()

    barrier = pltpu.get_barrier_semaphore()

    @pl.loop(1, n)
    def _(k):
        d = (me + k) % n
        pl.semaphore_signal(barrier, inc=1, device_id=(d // nz, d % nz), device_id_type=MESH)

    hot = pack_rows(nb, nz, sub, disp_ref, par_ref, bus_ref, pack)
    dloc.wait()
    pl.semaphore_wait(barrier, n - 1)

    def acopy(d, s):
        return pltpu.make_async_remote_copy(
            src_ref=pack.at[d], dst_ref=pin.at[s], send_sem=a_send.at[d], recv_sem=a_recv.at[s],
            device_id=(d // nz, d % nz), device_id_type=MESH,
        )

    @pl.loop(1, n)
    def _(k):
        acopy((me + k) % n, me).start()

    rows_of = (slice(0, half), slice(half, scen))

    def dcopy(m, h):
        to = flip(i, m, bits)
        return pltpu.make_async_remote_copy(
            src_ref=dem.at[i, rows_of[h]], dst_ref=dem.at[i, rows_of[h]],
            send_sem=dem_send.at[m, h], recv_sem=dem_recv.at[m, h],
            device_id=(to, j), device_id_type=MESH,
        )

    def dwait(m, h):
        o = flip(i, m, bits)
        return pltpu.make_async_remote_copy(
            src_ref=dem.at[o, rows_of[h]], dst_ref=dem.at[o, rows_of[h]],
            send_sem=dem_send.at[m, h], recv_sem=dem_recv.at[m, h],
            device_id=(o, j), device_id_type=MESH,
        )

    def fcopy(m, h):
        o = flip(i, m, bits)
        return pltpu.make_async_remote_copy(
            src_ref=dem.at[o, rows_of[h]], dst_ref=dem.at[o, rows_of[h]],
            send_sem=fw_send.at[m, h], recv_sem=fw_recv.at[m, h],
            device_id=(partner, j), device_id_type=MESH,
        )

    def fwait(m, h):
        o = flip(i, m + 1, bits)
        return pltpu.make_async_remote_copy(
            src_ref=dem.at[o, rows_of[h]], dst_ref=dem.at[o, rows_of[h]],
            send_sem=fw_send.at[m, h], recv_sem=fw_recv.at[m, h],
            device_id=(partner, j), device_id_type=MESH,
        )

    def relay_copy(m, h):
        o = flip(i, m, bits)
        return pltpu.make_async_remote_copy(
            src_ref=dem.at[o, rows_of[h]], dst_ref=dem.at[o, rows_of[h]],
            send_sem=rel_send.at[h], recv_sem=dem_recv.at[6, h],
            device_id=(flip(i, 6 - m, bits), j), device_id_type=MESH,
        )

    if relay:
        dcopy(2, 0).start()
        dcopy(4, 1).start()
        dcopy(2, 1).start()
        dcopy(4, 0).start()
    else:
        @pl.loop(1, nb // 2)
        def _(k):
            for h in range(2):
                dcopy(2 * k, h).start()

    for h in range(2):
        fcopy(0, h).start()

    @pl.loop(1, n)
    def _(k):
        s = (me + k) % n
        acopy(s, s).wait_recv()

    pin[me] = pack[me]
    if cap == ROWS:
        slots[...] = pin[...].reshape(s_count, LANES)
    else:
        for d in range(n):
            slots[d * cap:(d + 1) * cap, :] = pin[d, 0:cap, :]
    pack_t = slots[...].T
    lin = pack_t[scen:scen + 1, :]
    quad = pack_t[scen + 1:scen + 2, :]
    gmax = pack_t[scen + 2:scen + 3, :]
    dbuf[0, i] = pack_t[0:scen, :]

    def gcopy(it, m):
        to = flip(i, m, bits)
        return pltpu.make_async_remote_copy(
            src_ref=dbuf.at[it, i], dst_ref=dbuf.at[it, i],
            send_sem=d_send.at[it, m], recv_sem=d_recv.at[it, m],
            device_id=(to, j), device_id_type=MESH,
        )

    def gwait(it, m):
        o = flip(i, m, bits)
        return pltpu.make_async_remote_copy(
            src_ref=dbuf.at[it, o], dst_ref=dbuf.at[it, o],
            send_sem=d_send.at[it, m], recv_sem=d_recv.at[it, m],
            device_id=(o, j), device_id_type=MESH,
        )

    def gforward(it, m):
        o = flip(i, m, bits)
        return pltpu.make_async_remote_copy(
            src_ref=dbuf.at[it, o], dst_ref=dbuf.at[it, o],
            send_sem=df_send.at[it, m], recv_sem=d_recv.at[it, m + 1],
            device_id=(partner, j), device_id_type=MESH,
        )

    def gstart(it):
        @pl.loop(1, nb // 2)
        def _(k):
            gcopy(it, nb - 2 * k).start()

        gcopy(it, 1).start()

    gstart(0)
    lf[...] = jnp.zeros_like(lf)
    lane = lax.broadcasted_iota(jnp.int32, (s_count, LANES), 1)
    at_lane = lax.broadcasted_iota(jnp.int32, (s_count, kt), 1).astype(jnp.float32) + 1.0

    @pl.loop(0, nb)
    def _(m):
        o = flip(i, m, bits)

        if relay:
            @pl.when(m == 2)
            def _():
                dwait(2, 0).wait_recv()
                relay_copy(2, 0).start()
                dwait(4, 1).wait_recv()
                relay_copy(4, 1).start()
                dwait(2, 1).wait_recv()
                for h in range(2):
                    fcopy(2, h).start()

            @pl.when(m == 3)
            def _():
                dwait(4, 0).wait_recv()
                for h in range(2):
                    fcopy(4, h).start()

        else:
            @pl.when((m > 0) & (m % 2 == 0))
            def _():
                for h in range(2):
                    dwait(m, h).wait_recv()
                    fcopy(m, h).start()

        @pl.when(m == nb - 2)
        def _():
            @pl.loop(1, nb // 2)
            def _(k):
                gwait(0, 2 * k).wait_recv()
                gforward(0, 2 * k).start()

            if relay:
                for h in range(2):
                    dwait(6, h).wait_recv()
                    fcopy(6, h).start()

        @pl.when(m % 2 == 1)
        def _():
            for h in range(2):
                fwait(m - 1, h).wait_recv()

        pcopy(m).wait()
        codes = jnp.sum(jnp.where(lane == LANES - nb + o, slots[...], 0.0), axis=1, keepdims=True)
        for t in range(sub // kt):
            cols = slice(t * kt, (t + 1) * kt)
            ph, plo = split(pbuf[m % depth, :, cols])
            dh, dl = split(dem[o, :, cols])
            oh = jnp.where(at_lane == codes - float(t * kt), 1.0, 0.0).astype(jnp.bfloat16)
            one = dot(jnp.concatenate([dh, dl, oh], axis=0), ph, NT)
            two = dot(jnp.concatenate([dh, oh], axis=0), plo, NT)
            if t == 0:
                acc1[...] = one
                acc2[...] = two
            else:
                acc1[...] += one
                acc2[...] += two
        lf[...] += (acc1[scen:2 * scen, :] + acc2[0:scen, :]) + acc1[0:scen, :]
        ghi[o] = acc1[2 * scen:2 * scen + s_count, :].astype(jnp.bfloat16)
        glo[o] = acc2[scen:scen + s_count, :].astype(jnp.bfloat16)

        @pl.when(m + depth < nb)
        def _():
            pcopy(m + depth).start()

    price = lp0_ref[...]
    bound = dual_step * fmax_ref[...]

    for it in range(ITERS):
        zbuf[it, j] = -lf[...]

        def add_flow(m, it=it):
            o = flip(i, m, bits)
            dh, dl = split(dbuf[it, o])
            both = dot(jnp.concatenate([dh, dl], axis=0), ghi[o], NN)
            zbuf[it, j] += both[scen:, :] + dot(dh, glo[o], NN) + both[0:scen, :]

        add_flow(0)

        if it > 0:
            gwait(it, 1).wait_recv()
            add_flow(1)

            @pl.loop(1, nb // 2)
            def _(k, it=it):
                gwait(it, 2 * k).wait_recv()
                gforward(it, 2 * k).start()
                add_flow(2 * k)

            @pl.loop(1, nb // 2)
            def _(k, it=it):
                gwait(it, 2 * k + 1).wait_recv()
                add_flow(2 * k + 1)
        else:
            @pl.loop(1, nb)
            def _(m, it=it):
                @pl.when(m % 2 == 1)
                def _():
                    gwait(it, m).wait_recv()

                add_flow(m)

        def zcopy(k, it=it):
            to = (j + k) % nz
            return pltpu.make_async_remote_copy(
                src_ref=zbuf.at[it, j], dst_ref=zbuf.at[it, j],
                send_sem=z_send.at[it, k], recv_sem=z_recv.at[it, j],
                device_id=(i, to), device_id_type=MESH,
            )

        def zwait(k, it=it):
            o = (j + k) % nz
            return pltpu.make_async_remote_copy(
                src_ref=zbuf.at[it, o], dst_ref=zbuf.at[it, o],
                send_sem=z_send.at[it, k], recv_sem=z_recv.at[it, o],
                device_id=(i, o), device_id_type=MESH,
            )

        for k in range(1, nz):
            zcopy(k).start()
        for k in range(1, nz):
            zwait(k).wait_recv()
        flow = zbuf[it, 0]
        for k in range(1, nz):
            flow = flow + zbuf[it, k]
        trial = price + dual_step * flow
        price_next = trial - jnp.clip(trial, -bound, bound)
        reflected = 2.0 * price_next - price
        price = price_next

        rh, rl = split(reflected)
        rhl = jnp.concatenate([rh, rl], axis=0)

        def slot_price(o):
            both = dot(rhl, ghi[o], NT)
            return both[scen:, :] + dot(rh, glo[o], NT) + both[0:scen, :]

        def pxcopy(m, it=it):
            return pltpu.make_async_remote_copy(
                src_ref=pps.at[m], dst_ref=ppx.at[it, m // 2],
                send_sem=px_send.at[it, m // 2], recv_sem=px_recv.at[it, m // 2],
                device_id=(partner, j), device_id_type=MESH,
            )

        def ppcopy(m, it=it):
            o = flip(i, m, bits)
            return pltpu.make_async_remote_copy(
                src_ref=pps.at[m], dst_ref=ppr.at[it, m // 2],
                send_sem=pp_send.at[it, m // 2], recv_sem=pp_recv.at[it, m // 2],
                device_id=(o, j), device_id_type=MESH,
            )

        @pl.loop(0, nb // 2)
        def _(k):
            m = nb - 1 - 2 * k
            pps[m] = slot_price(flip(i, m, bits))
            pxcopy(m).start()

        @pl.loop(0, nb // 2 - 1)
        def _(k):
            m = nb - 2 - 2 * k
            term = slot_price(flip(i, m, bits))
            pxcopy(m + 1).wait_recv()
            pps[m] = term + ppx[it, m // 2]
            ppcopy(m).start()

        unit = slot_price(i)
        pxcopy(1).wait_recv()
        unit = unit + ppx[it, 0]
        for k in range(1, nb // 2):
            ppcopy(2 * k).wait_recv()
            unit = unit + ppr[it, k]
        for k in range(nb // 2):
            pxcopy(2 * k + 1).wait_send()
            if k:
                ppcopy(2 * k).wait_send()
        held = dbuf[it, i]
        held = jnp.clip(
            (held - primal_step * (lin + unit)) / (1.0 + primal_step * quad), 0.0, gmax
        )
        if it < ITERS - 1:
            dbuf[it + 1, i] = held
            gstart(it + 1)

    lp_ref[...] = price
    back = jnp.concatenate([held, jnp.zeros((LANES - scen, s_count), jnp.float32)], axis=0).T
    if cap == ROWS:
        rout[...] = back.reshape(n, ROWS, LANES)
    else:
        rout[...] = jnp.zeros_like(rout)
        slots[...] = back
        for d in range(n):
            rout[d, 0:cap, :] = slots[d * cap:(d + 1) * cap, :]

    def rcopy(d, s):
        return pltpu.make_async_remote_copy(
            src_ref=rout.at[d], dst_ref=rin.at[s], send_sem=r_send.at[d], recv_sem=r_recv.at[s],
            device_id=(d // nz, d % nz), device_id_type=MESH,
        )

    @pl.loop(1, n)
    def _(k):
        rcopy((me + k) % n, me).start()

    for h in range(2):
        fcopy(0, h).wait_send()
    if relay:
        relay_copy(2, 0).wait_send()
        relay_copy(4, 1).wait_send()
    direct = 2 if relay else nb // 2 - 1

    @pl.loop(1, nb // 2)
    def _(k):
        for h in range(2):
            fcopy(2 * k, h).wait_send()

            @pl.when(k <= direct)
            def _(h=h):
                dcopy(2 * k, h).wait_send()

        for it in range(ITERS):
            gcopy(it, 2 * k).wait_send()
            gforward(it, 2 * k).wait_send()

    for it in range(ITERS):
        gcopy(it, 1).wait_send()

    for it in range(ITERS):
        for k in range(1, nz):
            pltpu.make_async_remote_copy(
                src_ref=zbuf.at[it, j], dst_ref=zbuf.at[it, j],
                send_sem=z_send.at[it, k], recv_sem=z_recv.at[it, j],
                device_id=(i, (j + k) % nz), device_id_type=MESH,
            ).wait_send()

    rin[me] = rout[me]

    @pl.loop(1, n)
    def _(k):
        d = (me + k) % n
        acopy(d, d).wait_send()
        rcopy(d, d).wait_recv()
        rcopy(d, d).wait_send()

    home = rin[...].reshape(n * ROWS, LANES).T[0:scen, :]
    out_ref[...] = exact(home, hot, NN)


def exact(x, hot, dims):
    hi, lo = split(x)
    lo2 = (x - hi.astype(jnp.float32) - lo.astype(jnp.float32)).astype(jnp.bfloat16)
    return (dot(hi, hot, dims) + dot(lo, hot, dims)) + dot(lo2, hot, dims)


def pack_rows(nb, nz, sub, disp_ref, par_ref, bus_ref, pack):
    scen, gens = disp_ref.shape
    n = nb * nz
    f32, bf16 = jnp.float32, jnp.bfloat16
    bus = bus_ref[...].astype(f32)
    cell = jnp.floor((bus + 0.5) * (1.0 / sub))
    code = bus - cell * sub + 1.0
    block = jnp.floor((cell + 0.5) * (1.0 / nb))
    piece = cell - block * nb
    owner = piece * nz + block
    owner_col = jnp.broadcast_to(owner, (LANES, gens)).T[:, 0:1]
    same = owner_col == owner
    earlier = lax.broadcasted_iota(jnp.int32, (gens, gens), 0) < lax.broadcasted_iota(
        jnp.int32, (gens, gens), 1
    )
    rank = jnp.sum(jnp.where(same & earlier, 1.0, 0.0), axis=0, keepdims=True)
    row = lax.broadcasted_iota(jnp.int32, (n * ROWS, gens), 0)
    hot = jnp.where(row.astype(f32) == owner * ROWS + rank, 1.0, 0.0).astype(bf16)
    per = nz * ROWS
    hot_codes = jnp.where((row % per).astype(f32) == block * ROWS + rank, 1.0, 0.0).astype(bf16)
    holder = lax.broadcasted_iota(jnp.int32, (nb, gens), 0).astype(f32)
    codes = jnp.concatenate(
        [jnp.zeros((LANES - nb, gens), f32), jnp.where(holder == piece, code, 0.0)], axis=0
    )
    body = jnp.concatenate(
        [disp_ref[...], par_ref[...], jnp.zeros((LANES - scen - ROWS, gens), f32)], axis=0
    )
    hi, lo = split(body)
    lo2 = (body - hi.astype(f32) - lo.astype(f32)).astype(bf16)
    tile = (dot(hot, hi, NT) + dot(hot, lo, NT)) + dot(hot, lo2, NT)
    ch, cl = split(codes)
    tile = tile + (dot(hot_codes, ch, NT) + dot(hot_codes, cl, NT))
    pack[...] = tile.reshape(n, ROWS, LANES)
    return hot


def on_device(
    dispatch0, cost_lin, cost_quad, gen_max, bus_map, demand, ptdf, line_price0, flow_max
):
    nb = lax.axis_size("band")
    nz = lax.axis_size("bus")
    n = nb * nz
    gens = bus_map.shape[0]
    scen = dispatch0.shape[0]
    sub = demand.shape[2]
    lines = ptdf.shape[0]
    cap = (gens + n - 1) // n + 1
    while n * cap % LANES:
        cap += 1
    s_count = n * cap
    assert cap <= ROWS and scen + 4 + nb <= LANES and nb & (nb - 1) == 0
    params = jnp.stack([cost_lin, cost_quad, gen_max])
    params = jnp.pad(params, ((0, ROWS - params.shape[0]), (0, 0)))
    depth = min(nb, 8)
    kt = sub
    while kt > 1024:
        kt //= 2
    if sub % kt or kt % LANES:
        kt = sub
    if sub % 1024 == 0:
        kt = 1024
    f32, bf16 = jnp.float32, jnp.bfloat16
    anywhere = pl.BlockSpec(memory_space=pl.ANY)
    vmem = pl.BlockSpec(memory_space=pltpu.VMEM)
    dma = pltpu.SemaphoreType.DMA
    return pl.pallas_call(
        functools.partial(market_kernel, nb, nz, cap, depth, kt),
        out_shape=(
            jax.ShapeDtypeStruct((scen, gens), f32),
            jax.ShapeDtypeStruct((scen, lines), f32),
        ),
        in_specs=[vmem, vmem, vmem, anywhere, anywhere, vmem, vmem],
        out_specs=(vmem, vmem),
        scratch_shapes=[
            pltpu.VMEM((n, ROWS, LANES), f32),
            pltpu.VMEM((n, ROWS, LANES), f32),
            pltpu.VMEM((s_count, LANES), f32),
            pltpu.VMEM((nb, scen, sub), f32),
            pltpu.VMEM((depth, lines, sub), f32),
            pltpu.VMEM((2 * scen + s_count, lines), f32),
            pltpu.VMEM((scen + s_count, lines), f32),
            pltpu.VMEM((nb, s_count, lines), bf16),
            pltpu.VMEM((nb, s_count, lines), bf16),
            pltpu.VMEM((scen, lines), f32),
            pltpu.VMEM((ITERS, nz, scen, lines), f32),
            pltpu.VMEM((ITERS, nb, scen, s_count), f32),
            pltpu.VMEM((nb, scen, s_count), f32),
            pltpu.VMEM((ITERS, nb // 2, scen, s_count), f32),
            pltpu.VMEM((ITERS, nb // 2, scen, s_count), f32),
            pltpu.VMEM((n, ROWS, LANES), f32),
            pltpu.VMEM((n, ROWS, LANES), f32),
            dma((2,)), dma((depth,)),
            dma((n,)), dma((n,)),
            dma((nb, 2)), dma((nb, 2)), dma((nb, 2)), dma((nb, 2)), dma((2,)),
            dma((ITERS, nz)), dma((ITERS, nz)),
            dma((ITERS, nb)), dma((ITERS, nb)), dma((ITERS, nb)),
            dma((ITERS, nb // 2)), dma((ITERS, nb // 2)),
            dma((ITERS, nb // 2)), dma((ITERS, nb // 2)),
            dma((n,)), dma((n,)),
        ],
        compiler_params=pltpu.CompilerParams(
            collective_id=0, has_side_effects=True, vmem_limit_bytes=60 * 1024 * 1024
        ),
        name="market",
    )(dispatch0, params, bus_map[None, :], demand, ptdf, line_price0, flow_max[None, :])


def solution(mesh):
    in_specs = (
        P(None, ("band", "bus")),
        P(("band", "bus")),
        P(("band", "bus")),
        P(("band", "bus")),
        P(("band", "bus")),
        P(None, "bus", "band"),
        P("band", "bus"),
        P(None, "band"),
        P("band"),
    )
    out_specs = (P(None, ("band", "bus")), P(None, "band"))
    return jax.shard_map(
        on_device, mesh=mesh, in_specs=in_specs, out_specs=out_specs, check_vma=False
    )
```

```python
import functools
import jax
import jax.numpy as jnp
from jax import lax
from jax.experimental import pallas as pl
from jax.experimental.pallas import tpu as pltpu
from jax.sharding import PartitionSpec as P

ITERS = 2
ROWS = 8
LANES = 128
MESH = pl.DeviceIdType.MESH

primal_step = 0.5
dual_step = 1.0

NT = (((1,), (1,)), ((), ()))
NN = (((1,), (0,)), ((), ()))


def split(x):
    hi = x.astype(jnp.bfloat16)
    lo = (x - hi.astype(jnp.float32)).astype(jnp.bfloat16)
    return hi, lo


def dot(a, b, dims):
    return lax.dot_general(a, b, dims, preferred_element_type=jnp.float32)


def flip(i, m, bits):
    r = i
    for b in range(bits):
        w = 1 << b
        ib = (i // w) % 2
        mb = (m // w) % 2
        r = r + w * mb * (1 - 2 * ib)
    return r


def market_kernel(
    nb, nz, cap, depth, kt,
    disp_ref, par_ref, bus_ref, dem_ref, ptdf_ref, lp0_ref, fmax_ref,
    out_ref, lp_ref,
    pack, pin, slots, dem, pbuf, acc1, acc2, ghi, glo, lf, zbuf, dbuf, pps, ppx, ppr, rout, rin,
    dloc_sem, p_sem, a_send, a_recv, dem_send, dem_recv, fw_send, fw_recv, rel_send,
    z_send, z_recv, d_send, d_recv, df_send, px_send, px_recv, pp_send, pp_recv, r_send, r_recv,
):
    i = lax.axis_index("band")
    j = lax.axis_index("bus")
    n = nb * nz
    me = i * nz + j
    bits = nb.bit_length() - 1
    scen = lp0_ref.shape[0]
    lines = lp0_ref.shape[1]
    sub = dem_ref.shape[2]
    gens = disp_ref.shape[1]
    relay = nb == 8
    half = scen // 2
    s_count = n * cap
    partner = i + 1 - 2 * (i % 2)

    def pcopy(m):
        o = flip(i, m, bits)
        return pltpu.make_async_copy(
            ptdf_ref.at[:, pl.ds(pl.multiple_of(o * sub, LANES), sub)],
            pbuf.at[m % depth],
            p_sem.at[m % depth],
        )

    @pl.loop(0, depth)
    def _(m):
        pcopy(m).start()

    dloc = pltpu.make_async_copy(dem_ref.at[:, 0, :], dem.at[i], dloc_sem.at[0])
    dloc.start()

    barrier = pltpu.get_barrier_semaphore()

    @pl.loop(1, n)
    def _(k):
        d = (me + k) % n
        pl.semaphore_signal(barrier, inc=1, device_id=(d // nz, d % nz), device_id_type=MESH)

    hot = pack_rows(nb, nz, sub, disp_ref, par_ref, bus_ref, pack)
    dloc.wait()
    pl.semaphore_wait(barrier, n - 1)

    def acopy(d, s):
        return pltpu.make_async_remote_copy(
            src_ref=pack.at[d], dst_ref=pin.at[s], send_sem=a_send.at[d], recv_sem=a_recv.at[s],
            device_id=(d // nz, d % nz), device_id_type=MESH,
        )

    @pl.loop(1, n)
    def _(k):
        acopy((me + k) % n, me).start()

    rows_of = (slice(0, half), slice(half, scen))

    def dcopy(m, h):
        to = flip(i, m, bits)
        return pltpu.make_async_remote_copy(
            src_ref=dem.at[i, rows_of[h]], dst_ref=dem.at[i, rows_of[h]],
            send_sem=dem_send.at[m, h], recv_sem=dem_recv.at[m, h],
            device_id=(to, j), device_id_type=MESH,
        )

    def dwait(m, h):
        o = flip(i, m, bits)
        return pltpu.make_async_remote_copy(
            src_ref=dem.at[o, rows_of[h]], dst_ref=dem.at[o, rows_of[h]],
            send_sem=dem_send.at[m, h], recv_sem=dem_recv.at[m, h],
            device_id=(o, j), device_id_type=MESH,
        )

    def fcopy(m, h):
        o = flip(i, m, bits)
        return pltpu.make_async_remote_copy(
            src_ref=dem.at[o, rows_of[h]], dst_ref=dem.at[o, rows_of[h]],
            send_sem=fw_send.at[m, h], recv_sem=fw_recv.at[m, h],
            device_id=(partner, j), device_id_type=MESH,
        )

    def fwait(m, h):
        o = flip(i, m + 1, bits)
        return pltpu.make_async_remote_copy(
            src_ref=dem.at[o, rows_of[h]], dst_ref=dem.at[o, rows_of[h]],
            send_sem=fw_send.at[m, h], recv_sem=fw_recv.at[m, h],
            device_id=(partner, j), device_id_type=MESH,
        )

    def relay_copy(m, h):
        o = flip(i, m, bits)
        return pltpu.make_async_remote_copy(
            src_ref=dem.at[o, rows_of[h]], dst_ref=dem.at[o, rows_of[h]],
            send_sem=rel_send.at[h], recv_sem=dem_recv.at[6, h],
            device_id=(flip(i, 6 - m, bits), j), device_id_type=MESH,
        )

    if relay:
        dcopy(2, 0).start()
        dcopy(4, 1).start()
        dcopy(2, 1).start()
        dcopy(4, 0).start()
    else:
        @pl.loop(1, nb // 2)
        def _(k):
            for h in range(2):
                dcopy(2 * k, h).start()

    for h in range(2):
        fcopy(0, h).start()

    @pl.loop(1, n)
    def _(k):
        s = (me + k) % n
        acopy(s, s).wait_recv()

    pin[me] = pack[me]
    if cap == ROWS:
        slots[...] = pin[...].reshape(s_count, LANES)
    else:
        for d in range(n):
            slots[d * cap:(d + 1) * cap, :] = pin[d, 0:cap, :]
    pack_t = slots[...].T
    lin = pack_t[scen:scen + 1, :]
    quad = pack_t[scen + 1:scen + 2, :]
    gmax = pack_t[scen + 2:scen + 3, :]
    dbuf[0, i] = pack_t[0:scen, :]

    def gcopy(it, m, h):
        to = flip(i, m, bits)
        return pltpu.make_async_remote_copy(
            src_ref=dbuf.at[it, i, rows_of[h]], dst_ref=dbuf.at[it, i, rows_of[h]],
            send_sem=d_send.at[2 * it + h, m], recv_sem=d_recv.at[2 * it + h, m],
            device_id=(to, j), device_id_type=MESH,
        )

    def gwait(it, m, h):
        o = flip(i, m, bits)
        return pltpu.make_async_remote_copy(
            src_ref=dbuf.at[it, o, rows_of[h]], dst_ref=dbuf.at[it, o, rows_of[h]],
            send_sem=d_send.at[2 * it + h, m], recv_sem=d_recv.at[2 * it + h, m],
            device_id=(o, j), device_id_type=MESH,
        )

    def gforward(it, m, h):
        o = flip(i, m, bits)
        return pltpu.make_async_remote_copy(
            src_ref=dbuf.at[it, o, rows_of[h]], dst_ref=dbuf.at[it, o, rows_of[h]],
            send_sem=df_send.at[2 * it + h, m], recv_sem=d_recv.at[2 * it + h, m + 1],
            device_id=(partner, j), device_id_type=MESH,
        )

    def gstart(it, h):
        @pl.loop(1, nb // 2)
        def _(k):
            gcopy(it, nb - 2 * k, h).start()

        gcopy(it, 1, h).start()

    for h in range(2):
        gstart(0, h)

    def slot_flow(it, m, r):
        o = flip(i, m, bits)
        dh, dl = split(dbuf[it, o, r])
        both = dot(jnp.concatenate([dh, dl], axis=0), ghi[o], NN)
        size = both.shape[0] // 2
        return both[size:, :] + dot(dh, glo[o], NN) + both[0:size, :]

    every = slice(0, scen)
    lf[...] = jnp.zeros_like(lf)
    lane = lax.broadcasted_iota(jnp.int32, (s_count, LANES), 1)
    at_lane = lax.broadcasted_iota(jnp.int32, (s_count, kt), 1).astype(jnp.float32) + 1.0

    @pl.loop(0, nb)
    def _(m):
        o = flip(i, m, bits)

        if relay:
            @pl.when(m == 2)
            def _():
                dwait(2, 0).wait_recv()
                relay_copy(2, 0).start()
                dwait(4, 1).wait_recv()
                relay_copy(4, 1).start()
                dwait(2, 1).wait_recv()
                for h in range(2):
                    fcopy(2, h).start()

            @pl.when(m == 3)
            def _():
                dwait(4, 0).wait_recv()
                for h in range(2):
                    fcopy(4, h).start()

        else:
            @pl.when((m > 0) & (m % 2 == 0))
            def _():
                for h in range(2):
                    dwait(m, h).wait_recv()
                    fcopy(m, h).start()

        @pl.when(m == nb - 2)
        def _():
            @pl.loop(1, nb // 2)
            def _(k):
                for h in range(2):
                    gwait(0, 2 * k, h).wait_recv()
                    gforward(0, 2 * k, h).start()

            for h in range(2):
                gwait(0, 1, h).wait_recv()
            zbuf[0, j] = slot_flow(0, 0, every)

            @pl.loop(1, nb - 2)
            def _(q):
                @pl.when((q > 1) & (q % 2 == 1))
                def _():
                    for h in range(2):
                        gwait(0, q, h).wait_recv()

                zbuf[0, j] += slot_flow(0, q, every)

            if relay:
                for h in range(2):
                    dwait(6, h).wait_recv()
                    fcopy(6, h).start()

        @pl.when(m % 2 == 1)
        def _():
            for h in range(2):
                fwait(m - 1, h).wait_recv()

        pcopy(m).wait()
        codes = jnp.sum(jnp.where(lane == LANES - nb + o, slots[...], 0.0), axis=1, keepdims=True)
        for t in range(sub // kt):
            cols = slice(t * kt, (t + 1) * kt)
            ph, plo = split(pbuf[m % depth, :, cols])
            dh, dl = split(dem[o, :, cols])
            oh = jnp.where(at_lane == codes - float(t * kt), 1.0, 0.0).astype(jnp.bfloat16)
            one = dot(jnp.concatenate([dh, dl, oh], axis=0), ph, NT)
            two = dot(jnp.concatenate([dh, oh], axis=0), plo, NT)
            if t == 0:
                acc1[...] = one
                acc2[...] = two
            else:
                acc1[...] += one
                acc2[...] += two
        lf[...] += (acc1[scen:2 * scen, :] + acc2[0:scen, :]) + acc1[0:scen, :]
        ghi[o] = acc1[2 * scen:2 * scen + s_count, :].astype(jnp.bfloat16)
        glo[o] = acc2[scen:scen + s_count, :].astype(jnp.bfloat16)

        @pl.when(m + depth < nb)
        def _():
            pcopy(m + depth).start()

    bound = dual_step * fmax_ref[...]
    price = [lp0_ref[r, :] for r in rows_of]
    held = [None, None]

    def zcopy(it, k, h):
        to = (j + k) % nz
        return pltpu.make_async_remote_copy(
            src_ref=zbuf.at[it, j, rows_of[h]], dst_ref=zbuf.at[it, j, rows_of[h]],
            send_sem=z_send.at[2 * it + h, k], recv_sem=z_recv.at[2 * it + h, j],
            device_id=(i, to), device_id_type=MESH,
        )

    def zwait(it, k, h):
        o = (j + k) % nz
        return pltpu.make_async_remote_copy(
            src_ref=zbuf.at[it, o, rows_of[h]], dst_ref=zbuf.at[it, o, rows_of[h]],
            send_sem=z_send.at[2 * it + h, k], recv_sem=z_recv.at[2 * it + h, o],
            device_id=(i, o), device_id_type=MESH,
        )

    def pxcopy(it, m, h):
        return pltpu.make_async_remote_copy(
            src_ref=pps.at[m, rows_of[h]], dst_ref=ppx.at[it, m // 2, rows_of[h]],
            send_sem=px_send.at[2 * it + h, m // 2], recv_sem=px_recv.at[2 * it + h, m // 2],
            device_id=(partner, j), device_id_type=MESH,
        )

    def ppcopy(it, m, h):
        o = flip(i, m, bits)
        return pltpu.make_async_remote_copy(
            src_ref=pps.at[m, rows_of[h]], dst_ref=ppr.at[it, m // 2, rows_of[h]],
            send_sem=pp_send.at[2 * it + h, m // 2], recv_sem=pp_recv.at[2 * it + h, m // 2],
            device_id=(o, j), device_id_type=MESH,
        )

    def slot_price(o, ref):
        rh, rhl = ref
        both = dot(rhl, ghi[o], NT)
        return both[half:, :] + dot(rh, glo[o], NT) + both[0:half, :]

    for it in range(ITERS):
        if it == 0:
            for m in range(nb - 2, nb):
                for h in range(2):
                    if m % 2:
                        gwait(0, m, h).wait_recv()
                zbuf[0, j] += slot_flow(0, m, every)
            zbuf[0, j] -= lf[...]
            for h in range(2):
                for k in range(1, nz):
                    zcopy(0, k, h).start()
        else:
            for h in range(2):
                r = rows_of[h]
                zbuf[it, j, r] = slot_flow(it, 0, r) - lf[r, :]
                gwait(it, 1, h).wait_recv()
                zbuf[it, j, r] += slot_flow(it, 1, r)

                @pl.loop(1, nb // 2)
                def _(k, it=it, h=h, r=r):
                    gwait(it, 2 * k, h).wait_recv()
                    gforward(it, 2 * k, h).start()
                    zbuf[it, j, r] += slot_flow(it, 2 * k, r)

            for h in range(2):
                r = rows_of[h]

                @pl.loop(1, nb // 2)
                def _(k, it=it, h=h, r=r):
                    gwait(it, 2 * k + 1, h).wait_recv()
                    zbuf[it, j, r] += slot_flow(it, 2 * k + 1, r)

                for k in range(1, nz):
                    zcopy(it, k, h).start()

        moved = []
        for h in range(2):
            r = rows_of[h]
            for k in range(1, nz):
                zwait(it, k, h).wait_recv()
            flow = zbuf[it, 0, r]
            for k in range(1, nz):
                flow = flow + zbuf[it, k, r]
            trial = price[h] + dual_step * flow
            price_next = trial - jnp.clip(trial, -bound, bound)
            rh, rl = split(2.0 * price_next - price[h])
            price[h] = price_next
            moved.append((rh, jnp.concatenate([rh, rl], axis=0)))

            @pl.loop(0, nb // 2)
            def _(k, it=it, h=h, r=r, ref=moved[h]):
                m = nb - 1 - 2 * k
                pps[m, r] = slot_price(flip(i, m, bits), ref)
                pxcopy(it, m, h).start()

        for h in range(2):
            r = rows_of[h]

            @pl.loop(0, nb // 2 - 1)
            def _(k, it=it, h=h, r=r, ref=moved[h]):
                m = nb - 2 - 2 * k
                term = slot_price(flip(i, m, bits), ref)
                pxcopy(it, m + 1, h).wait_recv()
                pps[m, r] = term + ppx[it, m // 2, r]
                ppcopy(it, m, h).start()

        for h in range(2):
            r = rows_of[h]
            unit = slot_price(i, moved[h])
            pxcopy(it, 1, h).wait_recv()
            unit = unit + ppx[it, 0, r]
            for k in range(1, nb // 2):
                ppcopy(it, 2 * k, h).wait_recv()
                unit = unit + ppr[it, k, r]
            held[h] = jnp.clip(
                (dbuf[it, i, r] - primal_step * (lin + unit)) / (1.0 + primal_step * quad), 0.0, gmax
            )
            if it < ITERS - 1:
                dbuf[it + 1, i, r] = held[h]
                gstart(it + 1, h)

        for h in range(2):
            for k in range(nb // 2):
                pxcopy(it, 2 * k + 1, h).wait_send()
                if k:
                    ppcopy(it, 2 * k, h).wait_send()

    for h in range(2):
        lp_ref[rows_of[h], :] = price[h]
    back = jnp.concatenate([held[0], held[1], jnp.zeros((LANES - scen, s_count), jnp.float32)], axis=0).T
    if cap == ROWS:
        rout[...] = back.reshape(n, ROWS, LANES)
    else:
        rout[...] = jnp.zeros_like(rout)
        slots[...] = back
        for d in range(n):
            rout[d, 0:cap, :] = slots[d * cap:(d + 1) * cap, :]

    def rcopy(d, s):
        return pltpu.make_async_remote_copy(
            src_ref=rout.at[d], dst_ref=rin.at[s], send_sem=r_send.at[d], recv_sem=r_recv.at[s],
            device_id=(d // nz, d % nz), device_id_type=MESH,
        )

    @pl.loop(1, n)
    def _(k):
        rcopy((me + k) % n, me).start()

    for h in range(2):
        fcopy(0, h).wait_send()
    if relay:
        relay_copy(2, 0).wait_send()
        relay_copy(4, 1).wait_send()
    direct = 2 if relay else nb // 2 - 1

    @pl.loop(1, nb // 2)
    def _(k):
        for h in range(2):
            fcopy(2 * k, h).wait_send()

            @pl.when(k <= direct)
            def _(h=h):
                dcopy(2 * k, h).wait_send()

        for it in range(ITERS):
            for h in range(2):
                gcopy(it, 2 * k, h).wait_send()
                gforward(it, 2 * k, h).wait_send()

    for it in range(ITERS):
        for h in range(2):
            gcopy(it, 1, h).wait_send()
            for k in range(1, nz):
                zcopy(it, k, h).wait_send()

    rin[me] = rout[me]

    @pl.loop(1, n)
    def _(k):
        d = (me + k) % n
        acopy(d, d).wait_send()
        rcopy(d, d).wait_recv()
        rcopy(d, d).wait_send()

    home = rin[...].reshape(n * ROWS, LANES).T[0:scen, :]
    out_ref[...] = exact(home, hot, NN)


def exact(x, hot, dims):
    hi, lo = split(x)
    lo2 = (x - hi.astype(jnp.float32) - lo.astype(jnp.float32)).astype(jnp.bfloat16)
    return (dot(hi, hot, dims) + dot(lo, hot, dims)) + dot(lo2, hot, dims)


def pack_rows(nb, nz, sub, disp_ref, par_ref, bus_ref, pack):
    scen, gens = disp_ref.shape
    n = nb * nz
    f32, bf16 = jnp.float32, jnp.bfloat16
    bus = bus_ref[...].astype(f32)
    cell = jnp.floor((bus + 0.5) * (1.0 / sub))
    code = bus - cell * sub + 1.0
    block = jnp.floor((cell + 0.5) * (1.0 / nb))
    piece = cell - block * nb
    owner = piece * nz + block
    owner_col = jnp.broadcast_to(owner, (LANES, gens)).T[:, 0:1]
    same = owner_col == owner
    earlier = lax.broadcasted_iota(jnp.int32, (gens, gens), 0) < lax.broadcasted_iota(
        jnp.int32, (gens, gens), 1
    )
    rank = jnp.sum(jnp.where(same & earlier, 1.0, 0.0), axis=0, keepdims=True)
    row = lax.broadcasted_iota(jnp.int32, (n * ROWS, gens), 0)
    hot = jnp.where(row.astype(f32) == owner * ROWS + rank, 1.0, 0.0).astype(bf16)
    per = nz * ROWS
    hot_codes = jnp.where((row % per).astype(f32) == block * ROWS + rank, 1.0, 0.0).astype(bf16)
    holder = lax.broadcasted_iota(jnp.int32, (nb, gens), 0).astype(f32)
    codes = jnp.concatenate(
        [jnp.zeros((LANES - nb, gens), f32), jnp.where(holder == piece, code, 0.0)], axis=0
    )
    body = jnp.concatenate(
        [disp_ref[...], par_ref[...], jnp.zeros((LANES - scen - ROWS, gens), f32)], axis=0
    )
    hi, lo = split(body)
    lo2 = (body - hi.astype(f32) - lo.astype(f32)).astype(bf16)
    tile = (dot(hot, hi, NT) + dot(hot, lo, NT)) + dot(hot, lo2, NT)
    ch, cl = split(codes)
    tile = tile + (dot(hot_codes, ch, NT) + dot(hot_codes, cl, NT))
    pack[...] = tile.reshape(n, ROWS, LANES)
    return hot


def on_device(
    dispatch0, cost_lin, cost_quad, gen_max, bus_map, demand, ptdf, line_price0, flow_max
):
    nb = lax.axis_size("band")
    nz = lax.axis_size("bus")
    n = nb * nz
    gens = bus_map.shape[0]
    scen = dispatch0.shape[0]
    sub = demand.shape[2]
    lines = ptdf.shape[0]
    cap = (gens + n - 1) // n + 1
    while n * cap % LANES:
        cap += 1
    s_count = n * cap
    assert cap <= ROWS and scen + 4 + nb <= LANES and nb & (nb - 1) == 0
    params = jnp.stack([cost_lin, cost_quad, gen_max])
    params = jnp.pad(params, ((0, ROWS - params.shape[0]), (0, 0)))
    depth = min(nb, 8)
    kt = sub
    while kt > 1024:
        kt //= 2
    if sub % kt or kt % LANES:
        kt = sub
    if sub % 1024 == 0:
        kt = 1024
    f32, bf16 = jnp.float32, jnp.bfloat16
    anywhere = pl.BlockSpec(memory_space=pl.ANY)
    vmem = pl.BlockSpec(memory_space=pltpu.VMEM)
    dma = pltpu.SemaphoreType.DMA
    return pl.pallas_call(
        functools.partial(market_kernel, nb, nz, cap, depth, kt),
        out_shape=(
            jax.ShapeDtypeStruct((scen, gens), f32),
            jax.ShapeDtypeStruct((scen, lines), f32),
        ),
        in_specs=[vmem, vmem, vmem, anywhere, anywhere, vmem, vmem],
        out_specs=(vmem, vmem),
        scratch_shapes=[
            pltpu.VMEM((n, ROWS, LANES), f32),
            pltpu.VMEM((n, ROWS, LANES), f32),
            pltpu.VMEM((s_count, LANES), f32),
            pltpu.VMEM((nb, scen, sub), f32),
            pltpu.VMEM((depth, lines, sub), f32),
            pltpu.VMEM((2 * scen + s_count, lines), f32),
            pltpu.VMEM((scen + s_count, lines), f32),
            pltpu.VMEM((nb, s_count, lines), bf16),
            pltpu.VMEM((nb, s_count, lines), bf16),
            pltpu.VMEM((scen, lines), f32),
            pltpu.VMEM((ITERS, nz, scen, lines), f32),
            pltpu.VMEM((ITERS, nb, scen, s_count), f32),
            pltpu.VMEM((nb, scen, s_count), f32),
            pltpu.VMEM((ITERS, nb // 2, scen, s_count), f32),
            pltpu.VMEM((ITERS, nb // 2, scen, s_count), f32),
            pltpu.VMEM((n, ROWS, LANES), f32),
            pltpu.VMEM((n, ROWS, LANES), f32),
            dma((2,)), dma((depth,)),
            dma((n,)), dma((n,)),
            dma((nb, 2)), dma((nb, 2)), dma((nb, 2)), dma((nb, 2)), dma((2,)),
            dma((2 * ITERS, nz)), dma((2 * ITERS, nz)),
            dma((2 * ITERS, nb)), dma((2 * ITERS, nb)), dma((2 * ITERS, nb)),
            dma((2 * ITERS, nb // 2)), dma((2 * ITERS, nb // 2)),
            dma((2 * ITERS, nb // 2)), dma((2 * ITERS, nb // 2)),
            dma((n,)), dma((n,)),
        ],
        compiler_params=pltpu.CompilerParams(
            collective_id=0, has_side_effects=True, vmem_limit_bytes=60 * 1024 * 1024
        ),
        name="market",
    )(dispatch0, params, bus_map[None, :], demand, ptdf, line_price0, flow_max[None, :])


def solution(mesh):
    in_specs = (
        P(None, ("band", "bus")),
        P(("band", "bus")),
        P(("band", "bus")),
        P(("band", "bus")),
        P(("band", "bus")),
        P(None, "bus", "band"),
        P("band", "bus"),
        P(None, "band"),
        P("band"),
    )
    out_specs = (P(None, ("band", "bus")), P(None, "band"))
    return jax.shard_map(
        on_device, mesh=mesh, in_specs=in_specs, out_specs=out_specs, check_vma=False
    )
```

```python
import functools
import jax
import jax.numpy as jnp
from jax import lax
from jax.experimental import pallas as pl
from jax.experimental.pallas import tpu as pltpu
from jax.sharding import PartitionSpec as P

ITERS = 2
ROWS = 8
LANES = 128
MESH = pl.DeviceIdType.MESH

primal_step = 0.5
dual_step = 1.0

NT = (((1,), (1,)), ((), ()))
NN = (((1,), (0,)), ((), ()))


def split(x):
    hi = x.astype(jnp.bfloat16)
    lo = (x - hi.astype(jnp.float32)).astype(jnp.bfloat16)
    return hi, lo


def dot(a, b, dims):
    return lax.dot_general(a, b, dims, preferred_element_type=jnp.float32)


def flip(i, m, bits):
    r = i
    for b in range(bits):
        w = 1 << b
        ib = (i // w) % 2
        mb = (m // w) % 2
        r = r + w * mb * (1 - 2 * ib)
    return r


def market_kernel(
    nb, nz, cap, depth, kt,
    disp_ref, lin_ref, quad_ref, gmax_ref, bus_ref, dem_ref, ptdf_ref, lp0_ref, fmax_ref,
    out_ref, lp_ref,
    pack, pin, slots, dem, pbuf, acc1, acc2, ghi, glo, lf, zbuf, dbuf, pps, ppx, ppr, rout, rin,
    dloc_sem, p_sem, a_send, a_recv, dem_send, dem_recv, fw_send, fw_recv, rel_send,
    z_send, z_recv, d_send, d_recv, df_send, px_send, px_recv, pp_send, pp_recv, r_send, r_recv,
):
    i = lax.axis_index("band")
    j = lax.axis_index("bus")
    n = nb * nz
    me = i * nz + j
    bits = nb.bit_length() - 1
    scen = lp0_ref.shape[0]
    lines = lp0_ref.shape[1]
    sub = dem_ref.shape[2]
    gens = disp_ref.shape[1]
    relay = nb == 8
    half = scen // 2
    s_count = n * cap
    partner = i + 1 - 2 * (i % 2)

    def pcopy(m):
        o = flip(i, m, bits)
        return pltpu.make_async_copy(
            ptdf_ref.at[:, pl.ds(pl.multiple_of(o * sub, LANES), sub)],
            pbuf.at[m % depth],
            p_sem.at[m % depth],
        )

    @pl.loop(0, depth)
    def _(m):
        pcopy(m).start()

    dloc = pltpu.make_async_copy(dem_ref.at[:, 0, :], dem.at[i], dloc_sem.at[0])
    dloc.start()

    barrier = pltpu.get_barrier_semaphore()

    @pl.loop(1, n)
    def _(k):
        d = (me + k) % n
        pl.semaphore_signal(barrier, inc=1, device_id=(d // nz, d % nz), device_id_type=MESH)

    hot = pack_rows(nb, nz, sub, disp_ref, (lin_ref, quad_ref, gmax_ref), bus_ref, pack)
    dloc.wait()
    pl.semaphore_wait(barrier, n - 1)

    def acopy(d, s):
        return pltpu.make_async_remote_copy(
            src_ref=pack.at[d], dst_ref=pin.at[s], send_sem=a_send.at[d], recv_sem=a_recv.at[s],
            device_id=(d // nz, d % nz), device_id_type=MESH,
        )

    @pl.loop(1, n)
    def _(k):
        acopy((me + k) % n, me).start()

    rows_of = (slice(0, half), slice(half, scen))

    def dcopy(m, h):
        to = flip(i, m, bits)
        return pltpu.make_async_remote_copy(
            src_ref=dem.at[i, rows_of[h]], dst_ref=dem.at[i, rows_of[h]],
            send_sem=dem_send.at[m, h], recv_sem=dem_recv.at[m, h],
            device_id=(to, j), device_id_type=MESH,
        )

    def dwait(m, h):
        o = flip(i, m, bits)
        return pltpu.make_async_remote_copy(
            src_ref=dem.at[o, rows_of[h]], dst_ref=dem.at[o, rows_of[h]],
            send_sem=dem_send.at[m, h], recv_sem=dem_recv.at[m, h],
            device_id=(o, j), device_id_type=MESH,
        )

    def fcopy(m, h):
        o = flip(i, m, bits)
        return pltpu.make_async_remote_copy(
            src_ref=dem.at[o, rows_of[h]], dst_ref=dem.at[o, rows_of[h]],
            send_sem=fw_send.at[m, h], recv_sem=fw_recv.at[m, h],
            device_id=(partner, j), device_id_type=MESH,
        )

    def fwait(m, h):
        o = flip(i, m + 1, bits)
        return pltpu.make_async_remote_copy(
            src_ref=dem.at[o, rows_of[h]], dst_ref=dem.at[o, rows_of[h]],
            send_sem=fw_send.at[m, h], recv_sem=fw_recv.at[m, h],
            device_id=(partner, j), device_id_type=MESH,
        )

    def relay_copy(m, h):
        o = flip(i, m, bits)
        return pltpu.make_async_remote_copy(
            src_ref=dem.at[o, rows_of[h]], dst_ref=dem.at[o, rows_of[h]],
            send_sem=rel_send.at[h], recv_sem=dem_recv.at[6, h],
            device_id=(flip(i, 6 - m, bits), j), device_id_type=MESH,
        )

    if relay:
        dcopy(2, 0).start()
        dcopy(4, 1).start()
        dcopy(2, 1).start()
        dcopy(4, 0).start()
    else:
        @pl.loop(1, nb // 2)
        def _(k):
            for h in range(2):
                dcopy(2 * k, h).start()

    for h in range(2):
        fcopy(0, h).start()

    @pl.loop(1, n)
    def _(k):
        s = (me + k) % n
        acopy(s, s).wait_recv()

    pin[me] = pack[me]
    if cap == ROWS:
        slots[...] = pin[...].reshape(s_count, LANES)
    else:
        for d in range(n):
            slots[d * cap:(d + 1) * cap, :] = pin[d, 0:cap, :]
    pack_t = slots[...].T
    lin = pack_t[scen:scen + 1, :]
    quad = pack_t[scen + 1:scen + 2, :]
    gmax = pack_t[scen + 2:scen + 3, :]
    dbuf[0, i] = pack_t[0:scen, :]

    def gcopy(it, m, h):
        to = flip(i, m, bits)
        return pltpu.make_async_remote_copy(
            src_ref=dbuf.at[it, i, rows_of[h]], dst_ref=dbuf.at[it, i, rows_of[h]],
            send_sem=d_send.at[2 * it + h, m], recv_sem=d_recv.at[2 * it + h, m],
            device_id=(to, j), device_id_type=MESH,
        )

    def gwait(it, m, h):
        o = flip(i, m, bits)
        return pltpu.make_async_remote_copy(
            src_ref=dbuf.at[it, o, rows_of[h]], dst_ref=dbuf.at[it, o, rows_of[h]],
            send_sem=d_send.at[2 * it + h, m], recv_sem=d_recv.at[2 * it + h, m],
            device_id=(o, j), device_id_type=MESH,
        )

    def gforward(it, m, h):
        o = flip(i, m, bits)
        return pltpu.make_async_remote_copy(
            src_ref=dbuf.at[it, o, rows_of[h]], dst_ref=dbuf.at[it, o, rows_of[h]],
            send_sem=df_send.at[2 * it + h, m], recv_sem=d_recv.at[2 * it + h, m + 1],
            device_id=(partner, j), device_id_type=MESH,
        )

    def gstart(it, h):
        @pl.loop(1, nb // 2)
        def _(k):
            gcopy(it, nb - 2 * k, h).start()

        gcopy(it, 1, h).start()

    for h in range(2):
        gstart(0, h)

    def slot_flow(it, m, r):
        o = flip(i, m, bits)
        dh, dl = split(dbuf[it, o, r])
        both = dot(jnp.concatenate([dh, dl], axis=0), ghi[o], NN)
        size = both.shape[0] // 2
        return both[size:, :] + dot(dh, glo[o], NN) + both[0:size, :]

    every = slice(0, scen)
    lf[...] = jnp.zeros_like(lf)
    lane = lax.broadcasted_iota(jnp.int32, (s_count, LANES), 1)
    at_lane = lax.broadcasted_iota(jnp.int32, (s_count, kt), 1).astype(jnp.float32) + 1.0

    @pl.loop(0, nb)
    def _(m):
        o = flip(i, m, bits)

        if relay:
            @pl.when(m == 2)
            def _():
                dwait(2, 0).wait_recv()
                relay_copy(2, 0).start()
                dwait(4, 1).wait_recv()
                relay_copy(4, 1).start()
                dwait(2, 1).wait_recv()
                for h in range(2):
                    fcopy(2, h).start()

            @pl.when(m == 3)
            def _():
                dwait(4, 0).wait_recv()
                for h in range(2):
                    fcopy(4, h).start()

        else:
            @pl.when((m > 0) & (m % 2 == 0))
            def _():
                for h in range(2):
                    dwait(m, h).wait_recv()
                    fcopy(m, h).start()

        @pl.when(m == nb - 2)
        def _():
            @pl.loop(1, nb // 2)
            def _(k):
                for h in range(2):
                    gwait(0, 2 * k, h).wait_recv()
                    gforward(0, 2 * k, h).start()

            for h in range(2):
                gwait(0, 1, h).wait_recv()
            zbuf[0, j] = slot_flow(0, 0, every)

            @pl.loop(1, nb - 2)
            def _(q):
                @pl.when((q > 1) & (q % 2 == 1))
                def _():
                    for h in range(2):
                        gwait(0, q, h).wait_recv()

                zbuf[0, j] += slot_flow(0, q, every)

            if relay:
                for h in range(2):
                    dwait(6, h).wait_recv()
                    fcopy(6, h).start()

        @pl.when(m % 2 == 1)
        def _():
            for h in range(2):
                fwait(m - 1, h).wait_recv()

        pcopy(m).wait()
        codes = jnp.sum(jnp.where(lane == LANES - nb + o, slots[...], 0.0), axis=1, keepdims=True)
        for t in range(sub // kt):
            cols = slice(t * kt, (t + 1) * kt)
            ph, plo = split(pbuf[m % depth, :, cols])
            dh, dl = split(dem[o, :, cols])
            oh = jnp.where(at_lane == codes - float(t * kt), 1.0, 0.0).astype(jnp.bfloat16)
            one = dot(jnp.concatenate([dh, dl, oh], axis=0), ph, NT)
            two = dot(jnp.concatenate([dh, oh], axis=0), plo, NT)
            if t == 0:
                acc1[...] = one
                acc2[...] = two
            else:
                acc1[...] += one
                acc2[...] += two
        lf[...] += (acc1[scen:2 * scen, :] + acc2[0:scen, :]) + acc1[0:scen, :]
        ghi[o] = acc1[2 * scen:2 * scen + s_count, :].astype(jnp.bfloat16)
        glo[o] = acc2[scen:scen + s_count, :].astype(jnp.bfloat16)

        @pl.when(m + depth < nb)
        def _():
            pcopy(m + depth).start()

    bound = dual_step * fmax_ref[...]
    price = [lp0_ref[r, :] for r in rows_of]
    held = [None, None]

    def zcopy(it, k, h):
        to = (j + k) % nz
        return pltpu.make_async_remote_copy(
            src_ref=zbuf.at[it, j, rows_of[h]], dst_ref=zbuf.at[it, j, rows_of[h]],
            send_sem=z_send.at[2 * it + h, k], recv_sem=z_recv.at[2 * it + h, j],
            device_id=(i, to), device_id_type=MESH,
        )

    def zwait(it, k, h):
        o = (j + k) % nz
        return pltpu.make_async_remote_copy(
            src_ref=zbuf.at[it, o, rows_of[h]], dst_ref=zbuf.at[it, o, rows_of[h]],
            send_sem=z_send.at[2 * it + h, k], recv_sem=z_recv.at[2 * it + h, o],
            device_id=(i, o), device_id_type=MESH,
        )

    def pxcopy(it, m, h):
        return pltpu.make_async_remote_copy(
            src_ref=pps.at[m, rows_of[h]], dst_ref=ppx.at[it, m // 2, rows_of[h]],
            send_sem=px_send.at[2 * it + h, m // 2], recv_sem=px_recv.at[2 * it + h, m // 2],
            device_id=(partner, j), device_id_type=MESH,
        )

    def ppcopy(it, m, h):
        o = flip(i, m, bits)
        return pltpu.make_async_remote_copy(
            src_ref=pps.at[m, rows_of[h]], dst_ref=ppr.at[it, m // 2, rows_of[h]],
            send_sem=pp_send.at[2 * it + h, m // 2], recv_sem=pp_recv.at[2 * it + h, m // 2],
            device_id=(o, j), device_id_type=MESH,
        )

    def slot_price(o, ref):
        rh, rhl = ref
        both = dot(rhl, ghi[o], NT)
        return both[half:, :] + dot(rh, glo[o], NT) + both[0:half, :]

    for it in range(ITERS):
        if it == 0:
            for m in range(nb - 2, nb):
                for h in range(2):
                    if m % 2:
                        gwait(0, m, h).wait_recv()
                zbuf[0, j] += slot_flow(0, m, every)
            zbuf[0, j] -= lf[...]
            for h in range(2):
                for k in range(1, nz):
                    zcopy(0, k, h).start()
        else:
            for h in range(2):
                r = rows_of[h]
                zbuf[it, j, r] = slot_flow(it, 0, r) - lf[r, :]
                gwait(it, 1, h).wait_recv()
                zbuf[it, j, r] += slot_flow(it, 1, r)

                @pl.loop(1, nb // 2)
                def _(k, it=it, h=h, r=r):
                    gwait(it, 2 * k, h).wait_recv()
                    gforward(it, 2 * k, h).start()
                    zbuf[it, j, r] += slot_flow(it, 2 * k, r)

            for h in range(2):
                r = rows_of[h]

                @pl.loop(1, nb // 2)
                def _(k, it=it, h=h, r=r):
                    gwait(it, 2 * k + 1, h).wait_recv()
                    zbuf[it, j, r] += slot_flow(it, 2 * k + 1, r)

                for k in range(1, nz):
                    zcopy(it, k, h).start()

        moved = []
        for h in range(2):
            r = rows_of[h]
            for k in range(1, nz):
                zwait(it, k, h).wait_recv()
            flow = zbuf[it, 0, r]
            for k in range(1, nz):
                flow = flow + zbuf[it, k, r]
            trial = price[h] + dual_step * flow
            price_next = trial - jnp.clip(trial, -bound, bound)
            rh, rl = split(2.0 * price_next - price[h])
            price[h] = price_next
            moved.append((rh, jnp.concatenate([rh, rl], axis=0)))

            @pl.loop(0, nb // 2)
            def _(k, it=it, h=h, r=r, ref=moved[h]):
                m = nb - 1 - 2 * k
                pps[m, r] = slot_price(flip(i, m, bits), ref)
                pxcopy(it, m, h).start()

        for h in range(2):
            r = rows_of[h]

            @pl.loop(0, nb // 2 - 1)
            def _(k, it=it, h=h, r=r, ref=moved[h]):
                m = nb - 2 - 2 * k
                term = slot_price(flip(i, m, bits), ref)
                pxcopy(it, m + 1, h).wait_recv()
                pps[m, r] = term + ppx[it, m // 2, r]
                ppcopy(it, m, h).start()

        for h in range(2):
            r = rows_of[h]
            unit = slot_price(i, moved[h])
            pxcopy(it, 1, h).wait_recv()
            unit = unit + ppx[it, 0, r]
            for k in range(1, nb // 2):
                ppcopy(it, 2 * k, h).wait_recv()
                unit = unit + ppr[it, k, r]
            held[h] = jnp.clip(
                (dbuf[it, i, r] - primal_step * (lin + unit)) / (1.0 + primal_step * quad), 0.0, gmax
            )
            if it < ITERS - 1:
                dbuf[it + 1, i, r] = held[h]
                gstart(it + 1, h)

        for h in range(2):
            for k in range(nb // 2):
                pxcopy(it, 2 * k + 1, h).wait_send()
                if k:
                    ppcopy(it, 2 * k, h).wait_send()

    for h in range(2):
        lp_ref[rows_of[h], :] = price[h]
    back = jnp.concatenate([held[0], held[1], jnp.zeros((LANES - scen, s_count), jnp.float32)], axis=0).T
    if cap == ROWS:
        rout[...] = back.reshape(n, ROWS, LANES)
    else:
        rout[...] = jnp.zeros_like(rout)
        slots[...] = back
        for d in range(n):
            rout[d, 0:cap, :] = slots[d * cap:(d + 1) * cap, :]

    def rcopy(d, s):
        return pltpu.make_async_remote_copy(
            src_ref=rout.at[d], dst_ref=rin.at[s], send_sem=r_send.at[d], recv_sem=r_recv.at[s],
            device_id=(d // nz, d % nz), device_id_type=MESH,
        )

    @pl.loop(1, n)
    def _(k):
        rcopy((me + k) % n, me).start()

    for h in range(2):
        fcopy(0, h).wait_send()
    if relay:
        relay_copy(2, 0).wait_send()
        relay_copy(4, 1).wait_send()
    direct = 2 if relay else nb // 2 - 1

    @pl.loop(1, nb // 2)
    def _(k):
        for h in range(2):
            fcopy(2 * k, h).wait_send()

            @pl.when(k <= direct)
            def _(h=h):
                dcopy(2 * k, h).wait_send()

        for it in range(ITERS):
            for h in range(2):
                gcopy(it, 2 * k, h).wait_send()
                gforward(it, 2 * k, h).wait_send()

    for it in range(ITERS):
        for h in range(2):
            gcopy(it, 1, h).wait_send()
            for k in range(1, nz):
                zcopy(it, k, h).wait_send()

    rin[me] = rout[me]

    @pl.loop(1, n)
    def _(k):
        d = (me + k) % n
        acopy(d, d).wait_send()
        rcopy(d, d).wait_recv()
        rcopy(d, d).wait_send()

    home = rin[...].reshape(n * ROWS, LANES).T[0:scen, :]
    out_ref[...] = exact(home, hot, NN)


def exact(x, hot, dims):
    hi, lo = split(x)
    lo2 = (x - hi.astype(jnp.float32) - lo.astype(jnp.float32)).astype(jnp.bfloat16)
    return (dot(hi, hot, dims) + dot(lo, hot, dims)) + dot(lo2, hot, dims)


def pack_rows(nb, nz, sub, disp_ref, par_refs, bus_ref, pack):
    scen, gens = disp_ref.shape
    n = nb * nz
    f32, bf16 = jnp.float32, jnp.bfloat16
    bus = bus_ref[...].astype(f32)
    cell = jnp.floor((bus + 0.5) * (1.0 / sub))
    code = bus - cell * sub + 1.0
    block = jnp.floor((cell + 0.5) * (1.0 / nb))
    piece = cell - block * nb
    owner = piece * nz + block
    owner_col = jnp.broadcast_to(owner, (LANES, gens)).T[:, 0:1]
    same = owner_col == owner
    earlier = lax.broadcasted_iota(jnp.int32, (gens, gens), 0) < lax.broadcasted_iota(
        jnp.int32, (gens, gens), 1
    )
    rank = jnp.sum(jnp.where(same & earlier, 1.0, 0.0), axis=0, keepdims=True)
    row = lax.broadcasted_iota(jnp.int32, (n * ROWS, gens), 0)
    hot = jnp.where(row.astype(f32) == owner * ROWS + rank, 1.0, 0.0).astype(bf16)
    per = nz * ROWS
    hot_codes = jnp.where((row % per).astype(f32) == block * ROWS + rank, 1.0, 0.0).astype(bf16)
    holder = lax.broadcasted_iota(jnp.int32, (nb, gens), 0).astype(f32)
    codes = jnp.concatenate(
        [jnp.zeros((LANES - nb, gens), f32), jnp.where(holder == piece, code, 0.0)], axis=0
    )
    at_row = lax.broadcasted_iota(jnp.int32, (ROWS, gens), 0)
    par = jnp.zeros((ROWS, gens), f32)
    for k, ref in enumerate(par_refs):
        par = jnp.where(at_row == k, ref[...], par)
    body = jnp.concatenate(
        [disp_ref[...], par, jnp.zeros((LANES - scen - ROWS, gens), f32)], axis=0
    )
    hi, lo = split(body)
    lo2 = (body - hi.astype(f32) - lo.astype(f32)).astype(bf16)
    tile = (dot(hot, hi, NT) + dot(hot, lo, NT)) + dot(hot, lo2, NT)
    ch, cl = split(codes)
    tile = tile + (dot(hot_codes, ch, NT) + dot(hot_codes, cl, NT))
    pack[...] = tile.reshape(n, ROWS, LANES)
    return hot


def on_device(
    dispatch0, cost_lin, cost_quad, gen_max, bus_map, demand, ptdf, line_price0, flow_max
):
    nb = lax.axis_size("band")
    nz = lax.axis_size("bus")
    n = nb * nz
    gens = bus_map.shape[0]
    scen = dispatch0.shape[0]
    sub = demand.shape[2]
    lines = ptdf.shape[0]
    cap = (gens + n - 1) // n + 1
    while n * cap % LANES:
        cap += 1
    s_count = n * cap
    assert cap <= ROWS and scen + 4 + nb <= LANES and nb & (nb - 1) == 0
    depth = min(nb, 8)
    kt = sub
    while kt > 1024:
        kt //= 2
    if sub % kt or kt % LANES:
        kt = sub
    if sub % 1024 == 0:
        kt = 1024
    f32, bf16 = jnp.float32, jnp.bfloat16
    anywhere = pl.BlockSpec(memory_space=pl.ANY)
    vmem = pl.BlockSpec(memory_space=pltpu.VMEM)
    dma = pltpu.SemaphoreType.DMA
    return pl.pallas_call(
        functools.partial(market_kernel, nb, nz, cap, depth, kt),
        out_shape=(
            jax.ShapeDtypeStruct((scen, gens), f32),
            jax.ShapeDtypeStruct((scen, lines), f32),
        ),
        in_specs=[vmem, vmem, vmem, vmem, vmem, anywhere, anywhere, vmem, vmem],
        out_specs=(vmem, vmem),
        scratch_shapes=[
            pltpu.VMEM((n, ROWS, LANES), f32),
            pltpu.VMEM((n, ROWS, LANES), f32),
            pltpu.VMEM((s_count, LANES), f32),
            pltpu.VMEM((nb, scen, sub), f32),
            pltpu.VMEM((depth, lines, sub), f32),
            pltpu.VMEM((2 * scen + s_count, lines), f32),
            pltpu.VMEM((scen + s_count, lines), f32),
            pltpu.VMEM((nb, s_count, lines), bf16),
            pltpu.VMEM((nb, s_count, lines), bf16),
            pltpu.VMEM((scen, lines), f32),
            pltpu.VMEM((ITERS, nz, scen, lines), f32),
            pltpu.VMEM((ITERS, nb, scen, s_count), f32),
            pltpu.VMEM((nb, scen, s_count), f32),
            pltpu.VMEM((ITERS, nb // 2, scen, s_count), f32),
            pltpu.VMEM((ITERS, nb // 2, scen, s_count), f32),
            pltpu.VMEM((n, ROWS, LANES), f32),
            pltpu.VMEM((n, ROWS, LANES), f32),
            dma((2,)), dma((depth,)),
            dma((n,)), dma((n,)),
            dma((nb, 2)), dma((nb, 2)), dma((nb, 2)), dma((nb, 2)), dma((2,)),
            dma((2 * ITERS, nz)), dma((2 * ITERS, nz)),
            dma((2 * ITERS, nb)), dma((2 * ITERS, nb)), dma((2 * ITERS, nb)),
            dma((2 * ITERS, nb // 2)), dma((2 * ITERS, nb // 2)),
            dma((2 * ITERS, nb // 2)), dma((2 * ITERS, nb // 2)),
            dma((n,)), dma((n,)),
        ],
        compiler_params=pltpu.CompilerParams(
            collective_id=0, has_side_effects=True, vmem_limit_bytes=60 * 1024 * 1024
        ),
        name="market",
    )(
        dispatch0, cost_lin[None, :], cost_quad[None, :], gen_max[None, :], bus_map[None, :],
        demand, ptdf, line_price0, flow_max[None, :])


def solution(mesh):
    in_specs = (
        P(None, ("band", "bus")),
        P(("band", "bus")),
        P(("band", "bus")),
        P(("band", "bus")),
        P(("band", "bus")),
        P(None, "bus", "band"),
        P("band", "bus"),
        P(None, "band"),
        P("band"),
    )
    out_specs = (P(None, ("band", "bus")), P(None, "band"))
    return jax.shard_map(
        on_device, mesh=mesh, in_specs=in_specs, out_specs=out_specs, check_vma=False
    )
```
